32 devices in a mesh: bond: 8 (over z, x), mpo: 4 (over y, core).
Axes of the slice: x: 2, y: 2, z: 4, core: 2. Of those that a mesh axis runs over, the one named last changes fastest.
Arguments:
- wave_blocks: bfloat16 [8, 16, 256, 256], P('bond'), may hold values from -6 to 6
- left_environment: bfloat16 [8, 8, 256, 256], P('mpo', 'bond'), may hold values from -0.375 to 0.375
- right_environment: bfloat16 [8, 8, 256, 256], P('mpo', 'bond'), may hold values from -0.375 to 0.375
- site_operators: bfloat16 [8, 16, 16], P('mpo'), may hold values from -1.1953125 to 1.1953125
- right_sector: int32 [8, 16, 1], P('bond'), may hold values from 0 to 7; in each aligned block of 16 rows (0 to 15, 16 to 31, ..., all dimensions but the last counted through in order) at most 2 rows name the same one
- left_sizes: int32 [8], replicated, may hold values from 128 to 256
- right_sizes: int32 [8], replicated, may hold values from 128 to 256
- sector_place: int32 [8], replicated, may hold values from 0 to 7, each once
Outputs:
- applied: bfloat16 [8, 16, 256, 256], P('bond', 'mpo')
The draws below stay inside these ranges and needn't reach their ends.
Inputs may be any that keep to these rules, and one draw needn't show every extreme that they name: `right_sector`: among the 16 blocks of one bond index no right sector is named more than 2 times, a bound that some block reaches. `sector_place`: every position is taken by exactly one right sector.
All inputs are finite; a program needn't handle non-finite values.
Results may differ from the reference program's by a relative error of at most 0.0057.
Values may be sent and summed in bfloat16 or wider, within the bound.
A program may use at most 64 MiB of HBM per device.

```python
import math
import jax
import jax.numpy as jnp
import numpy as np
from jax import lax

SB = 256
P_SIZE = 16
CAPP = 2
NSD = 1
WM = 8
NS = 8


def touch_ends(array, own_key, smallest, top_value):
    index_at = [jax.random.randint(jax.random.fold_in(own_key, axis), (), 0, length) for axis, length in enumerate(array.shape)]
    widest = array.shape.index(max(array.shape))
    neighbour = index_at[:widest] + [(index_at[widest] + 1) % array.shape[widest]] + index_at[widest + 1:]
    return array.at[tuple(index_at)].set(smallest).at[tuple(neighbour)].set(top_value)


def levels(rng, extent, cuts, low, largest):
    def one(dim, parts):
        heights = jax.random.uniform(jax.random.fold_in(jax.random.fold_in(rng, 6), dim), (parts,), jnp.float32, low / len(cuts), largest / len(cuts))
        return jnp.repeat(jnp.exp(heights), extent[dim] // parts).reshape((-1,) + (1,) * (len(extent) - dim - 1))

    gain = one(*cuts[0])
    for cut in cuts[1:]:
        gain = gain * one(*cut)
    return gain


def shared_out(stream_key, own, number, rows, number_of, top, reach, skew):
    ranking = jax.random.permutation(stream_key, number_of)
    crowded, ordinary = portions_of(number_of, rows * top, reach, skew, True), portions_of(number_of, rows * top, reach, skew, False)
    places = jnp.arange(number_of)

    def named(tallies, turn):
        used = int((tallies > 0).sum())
        fixed = max(1, used // 4)
        shifted = fixed + (places - fixed + turn * (used - fixed)) % max(1, number_of - fixed)
        return jnp.zeros((number_of,), jnp.int32).at[ranking[jnp.where(places < fixed, places, shifted)]].set(jnp.asarray(tallies, jnp.int32))

    tallies = jnp.where(number % 4 == 0, named(crowded, number // 4), named(ordinary, number - number // 4 - 1))
    mixed = jax.random.permutation(jax.random.fold_in(own, 3), number_of)
    donor, receiver = mixed[0:number_of // 2 * 2:2], mixed[1:number_of // 2 * 2:2]
    slack = jnp.minimum(tallies[donor] - 1, reach - tallies[receiver]) // 2
    slack = jnp.where((donor == ranking[0]) | (receiver == ranking[0]) | (tallies[receiver] == 0), 0, jnp.maximum(slack, 0))
    shifted = jax.random.randint(jax.random.fold_in(own, 4), (number_of // 2,), 0, 1 << 20) % (slack + 1)
    tallies = tallies.at[donor].add(-shifted).at[receiver].add(shifted)
    labels = jnp.searchsorted(jnp.cumsum(tallies), jnp.arange(rows * top), side="right").astype(jnp.int32)
    listing = labels.reshape(top, rows).T
    listing = listing[jax.random.permutation(jax.random.fold_in(own, 1), rows)]
    turn = jax.random.randint(jax.random.fold_in(own, 2), (rows, 1), 0, top)
    return jnp.take_along_axis(listing, (jnp.arange(top)[None, :] + turn) % top, axis=1)


def portions_of(number_of, total, limit, slope, full):
    loads = [(1 << 20) // math.isqrt(grade ** slope) + 1 for grade in range(1, number_of + 1)]
    largest = limit if full else min(limit, max(-(-total // number_of), total * loads[0] // sum(loads)))
    least = 1 if total - largest >= number_of - 1 else 0
    given, spare = [largest] + [least] * (number_of - 1), total - largest - least * (number_of - 1)
    while spare > 0:
        free = [i for i in range(1, number_of) if given[i] < largest] or [i for i in range(1, number_of) if given[i] < limit]
        whole, remaining = sum([loads[i] for i in free]), spare
        for i in free:
            addition = min(limit - given[i], max(1, remaining * loads[i] // whole), spare)
            given[i] = given[i] + addition
            spare = spare - addition
    return np.array(given)


def normal_values(own_key, dims, scale, bound, pieces=(), kind=jnp.bfloat16):
    factor_of = levels(own_key, dims, pieces, -0.22, 0.18) if pieces else 1.0
    entries = jax.random.normal(own_key, dims, jnp.float32) * scale * factor_of
    return jnp.minimum(jnp.maximum(entries, -bound), bound).astype(kind)


def setup_inputs(seed: int = 0) -> dict:
    arg_keys = jax.random.split(jax.random.key(seed), 9)
    wave_blocks = normal_values(arg_keys[0], (NS, P_SIZE, SB, SB), 1.0, 6.0, ((0, 8),))
    left_environment = normal_values(arg_keys[1], (WM, NS, SB, SB), SB ** -0.5, 0.375, ((0, 4), (1, 8)))
    right_environment = normal_values(arg_keys[2], (WM, NS, SB, SB), SB ** -0.5, 0.375, ((0, 4), (1, 8)))
    site_operators = normal_values(arg_keys[3], (WM, P_SIZE, P_SIZE), 0.2, 1.1953125, ((0, 4),))
    right_sector_keys = jax.random.split(jax.random.fold_in(arg_keys[4], 1), NS * P_SIZE // (NSD * P_SIZE))
    right_sector_turns = jax.random.permutation(jax.random.fold_in(arg_keys[4], 3), NS * P_SIZE // (NSD * P_SIZE))
    right_sector = jax.vmap(lambda own, number: shared_out(jax.random.fold_in(arg_keys[4], 2), own, number, NSD * P_SIZE, NS, 1, CAPP, 2))(right_sector_keys, right_sector_turns).reshape((NS, P_SIZE, 1))
    left_sizes = touch_ends(jax.random.randint(arg_keys[5], (NS,), SB // 2, SB + 1), jax.random.fold_in(arg_keys[5], 1), SB // 2, SB).astype(jnp.int32)
    right_sizes = touch_ends(jax.random.randint(arg_keys[6], (NS,), SB // 2, SB + 1), jax.random.fold_in(arg_keys[6], 1), SB // 2, SB).astype(jnp.int32)
    sector_place = jax.random.permutation(arg_keys[7], NS).astype(jnp.int32)
    return {"wave_blocks": wave_blocks, "left_environment": left_environment, "right_environment": right_environment, "site_operators": site_operators, "right_sector": right_sector, "left_sizes": left_sizes, "right_sizes": right_sizes, "sector_place": sector_place}


def reference(wave_blocks, left_environment, right_environment, site_operators, right_sector, left_sizes, right_sizes, sector_place):
    sector_ids = right_sector[:, :, 0]
    offsets = jnp.arange(SB, dtype=jnp.int32)
    row_mask = offsets[None, :] < left_sizes[:, None]
    column_mask = offsets[None, None, :] < right_sizes[sector_ids][:, :, None]
    live_mask = row_mask[:, None, :, None] & column_mask[:, :, None, :]
    masked = jnp.where(live_mask, wave_blocks, jnp.zeros((), jnp.bfloat16))
    position = sector_place[sector_ids]
    same_sector = sector_ids[:, :, None] == sector_ids[:, None, :]
    masked_wide = masked.astype(jnp.float32)

    def one_channel(channel, running):
        chosen = jnp.take(right_environment[channel], position, axis=0).astype(jnp.float32)
        right_part = jnp.einsum('ksac,ksxc->ksax', masked_wide, chosen).astype(jnp.bfloat16)
        mixing = jnp.where(same_sector, site_operators[channel][None], jnp.zeros((), jnp.bfloat16))
        mixed = jnp.einsum('kst,ktac->ksac', mixing.astype(jnp.float32), right_part.astype(jnp.float32)).astype(jnp.bfloat16)
        return running + jnp.einsum('kab,ksbc->ksac', left_environment[channel].astype(jnp.float32), mixed.astype(jnp.float32))

    running = lax.fori_loop(0, WM, one_channel, jnp.zeros(wave_blocks.shape, jnp.float32))
    return jnp.where(live_mask, running, jnp.zeros((), jnp.float32)).astype(jnp.bfloat16)
```

```python
import functools

import jax
import jax.numpy as jnp
from jax import lax
from jax.experimental import pallas as pl
from jax.experimental.pallas import tpu as pltpu
from jax.sharding import PartitionSpec as P

MESH = pl.DeviceIdType.MESH


def plane_of(count):
    nx = 1
    while (2 * nx) * (2 * nx) * 2 <= count and count % (2 * nx) == 0:
        nx *= 2
    return count // nx, nx


def kernel(
    n, m,
    sector, place, left_sizes, right_sizes, ops,
    wave_hbm, left_hbm, right_hbm,
    out_ref,
    right_all, wave, left, mixed, out_core, in_core, out_chip, in_chip, own,
    local_sem, gather_send, gather_recv, core_send, core_recv, chip_send, chip_recv,
):
    nz, nx = plane_of(n)
    cores = 2 if m % 2 == 0 else 1
    ny = m // cores
    states, rows, _ = wave.shape
    channels = left.shape[0]
    per = out_ref.shape[0]
    count = ny * per
    b = lax.axis_index("bond")
    p = lax.axis_index("mpo")
    z, x = b // nx, b % nx
    y, c = p // cores, p % cores
    sibling = y * cores + (1 - c)

    wave_copy = pltpu.make_async_copy(wave_hbm, wave, local_sem.at[0])
    left_copy = pltpu.make_async_copy(left_hbm, left, local_sem.at[1])
    own_copy = pltpu.make_async_copy(right_hbm, right_all.at[b], local_sem.at[2])
    wave_copy.start()
    left_copy.start()
    own_copy.start()

    steps = ((nx, z + 1 < nz), (-nx, z > 0), (1, x + 1 < nx), (-1, x > 0))
    barrier = pltpu.get_barrier_semaphore()
    greeted = ny
    for step, there in steps:
        greeted = greeted + there.astype(jnp.int32)

        @pl.when(there)
        def _():
            pl.semaphore_signal(barrier, inc=1, device_id=(b + step, p), device_id_type=MESH)

    pl.semaphore_signal(barrier, inc=1, device_id=(b, sibling), device_id_type=MESH)
    for dy in range(1, ny):
        other = lax.rem(y + dy, ny) * cores + c
        pl.semaphore_signal(barrier, inc=1, device_id=(b, other), device_id_type=MESH)
    pl.semaphore_wait(barrier, greeted)

    def hop(pos, h, k, src):
        return pltpu.make_async_remote_copy(
            src_ref=src,
            dst_ref=right_all.at[pos, h],
            send_sem=gather_send.at[pos, h, k],
            recv_sem=gather_recv.at[pos, h],
            device_id=(b + steps[k][0], p),
            device_id_type=MESH,
        )

    def sends(zs, xs):
        column = xs == x
        return (
            column & (zs <= z) & (z + 1 < nz),
            column & (zs >= z) & (z > 0),
            (xs <= x) & (x + 1 < nx),
            (xs >= x) & (x > 0),
        )

    def forward(zs, xs, h):
        pos = zs * nx + xs
        for k, wanted in enumerate(sends(zs, xs)):
            @pl.when(wanted)
            def _():
                hop(pos, h, k, right_all.at[pos, h]).start()

    def arrived(pos, h):
        hop(pos, h, 0, right_all.at[pos, h]).wait_recv()

    for h in range(channels):
        for k in (0, 1, 2, 3):
            @pl.when(steps[k][1])
            def _():
                hop(b, h, k, right_hbm.at[h]).start()

    wave_copy.wait()
    left_copy.wait()
    own_copy.wait()

    row_index = lax.broadcasted_iota(jnp.int32, (rows, rows), 0)
    column_index = lax.broadcasted_iota(jnp.int32, (rows, rows), 1)
    live_rows = row_index < left_sizes[b]

    def work(pos):
        def look(s, carry):
            first, last, hits = carry
            hit = place[sector[s]] == pos
            first = jnp.where(hit & (hits == 0), s, first)
            last = jnp.where(hit, s, last)
            return first, last, hits + hit.astype(jnp.int32)

        zero = jnp.int32(0)
        s1, s2, hits = lax.fori_loop(0, states, look, (zero, zero, zero), unroll=True)
        live = live_rows & (column_index < right_sizes[sector[s1]])

        def masked(s):
            return jnp.where(live, wave[s].astype(jnp.float32), 0.0).astype(jnp.bfloat16)

        w1, w2 = masked(s1), masked(s2)
        two = hits == 2
        for h in range(channels):
            factor = right_all[pos, h]

            def right_part(w):
                part = lax.dot_general(
                    w, factor, (((1,), (1,)), ((), ())), preferred_element_type=jnp.float32
                )
                return part.astype(jnp.bfloat16).astype(jnp.float32)

            def op(s, t):
                return ops[(h * states + s) * states + t]

            p1, p2 = right_part(w1), right_part(w2)
            o12, o21 = jnp.where(two, op(s1, s2), 0.0), jnp.where(two, op(s2, s1), 0.0)
            mixed[2 * pos, h] = (op(s1, s1) * p1 + o12 * p2).astype(jnp.bfloat16)
            mixed[2 * pos + 1, h] = (o21 * p1 + op(s2, s2) * p2).astype(jnp.bfloat16)

    def gather_round(d, _):
        @pl.when((d > 0) & (d < nz))
        def _():
            for h in range(channels):
                for sign in (1, -1):
                    zs = z + sign * d

                    @pl.when((zs >= 0) & (zs < nz))
                    def _():
                        arrived(zs * nx + x, h)
                        forward(zs, x, h)

        def one(i, _):
            sign = 1 - 2 * (i % 2)
            e = i // 2
            offset = (e + 1) // 2 * (1 - 2 * (e % 2))
            zs = z + sign * (d - 1)
            xs = x + offset

            @pl.when((zs >= 0) & (zs < nz) & (xs >= 0) & (xs < nx) & ((d > 1) | (sign > 0)))
            def _():
                pos = zs * nx + xs

                @pl.when(xs != x)
                def _():
                    for h in range(channels):
                        arrived(pos, h)
                        forward(zs, xs, h)

                work(pos)

            return 0

        @pl.when(d > 0)
        def _():
            lax.fori_loop(0, 2 * (2 * nx - 1), one, 0)

        return 0

    lax.fori_loop(1, nz + 1, gather_round, 0)

    def product(s):
        def look(t, rank):
            return rank + ((t < s) & (sector[t] == sector[s])).astype(jnp.int32)

        rank = lax.fori_loop(0, states, look, jnp.int32(0), unroll=True)
        slot = 2 * place[sector[s]] + rank
        total = jnp.dot(left[0], mixed[slot, 0], preferred_element_type=jnp.float32)
        for h in range(1, channels):
            total += jnp.dot(left[h], mixed[slot, h], preferred_element_type=jnp.float32)
        return total

    def owner_chip(i):
        return lax.rem(y + 1 + i // per, ny)

    def to_core(i):
        return pltpu.make_async_remote_copy(
            src_ref=out_core.at[i], dst_ref=in_core.at[i],
            send_sem=core_send.at[i], recv_sem=core_recv.at[i],
            device_id=(b, sibling), device_id_type=MESH,
        )

    def to_chip(i):
        return pltpu.make_async_remote_copy(
            src_ref=out_chip.at[i], dst_ref=in_chip.at[i],
            send_sem=chip_send.at[i], recv_sem=chip_recv.at[i],
            device_id=(b, owner_chip(i) * cores + c), device_id_type=MESH,
        )

    remote = (ny - 1) * per
    lag = min(3, count)

    def reduce_step(i, _):
        @pl.when(i < count)
        def _():
            s = (owner_chip(i) * cores + (1 - c)) * per + i % per
            out_core[i] = product(s).astype(jnp.bfloat16)
            to_core(i).start()

        @pl.when(i >= lag)
        def _():
            j = i - lag
            s = (owner_chip(j) * cores + c) * per + j % per
            total = product(s)
            to_core(j).wait_recv()
            total = total + in_core[j].astype(jnp.float32)

            @pl.when(j < remote)
            def _():
                out_chip[j] = total.astype(jnp.bfloat16)
                to_chip(j).start()

            @pl.when(j >= remote)
            def _():
                own[j - remote] = total

        return 0

    lax.fori_loop(0, count + lag, reduce_step, 0)

    for q in range(per):
        total = own[q]
        for dy in range(ny - 1):
            to_chip(dy * per + q).wait_recv()
            total = total + in_chip[dy * per + q].astype(jnp.float32)
        live = live_rows & (column_index < right_sizes[sector[p * per + q]])
        out_ref[q] = jnp.where(live, total, 0.0).astype(jnp.bfloat16)

    def finish(pos, _):
        for k, wanted in enumerate(sends(pos // nx, pos % nx)):
            @pl.when(wanted)
            def _():
                for h in range(channels):
                    hop(pos, h, k, right_all.at[pos, h]).wait_send()
        return 0

    lax.fori_loop(0, n, finish, 0)

    def finish_core(i, _):
        to_core(i).wait_send()
        return 0

    lax.fori_loop(0, count, finish_core, 0)

    def finish_chip(i, _):
        to_chip(i).wait_send()
        return 0

    lax.fori_loop(0, remote, finish_chip, 0)


def shards(n, m, wave_blocks, left_environment, right_environment, site_operators,
           right_sector, left_sizes, right_sizes, sector_place):
    states, rows = wave_blocks.shape[1:3]
    channels = left_environment.shape[0]
    per = states // m
    cores = 2 if m % 2 == 0 else 1
    ny = m // cores
    count = ny * per
    remote = max(1, (ny - 1) * per)
    block = (rows, rows)
    bf16, f32 = jnp.bfloat16, jnp.float32
    smem = pl.BlockSpec(memory_space=pltpu.SMEM)
    hbm = pl.BlockSpec(memory_space=pl.ANY)
    out = pl.pallas_call(
        functools.partial(kernel, n, m),
        out_shape=jax.ShapeDtypeStruct((per,) + block, bf16),
        in_specs=[smem] * 5 + [hbm] * 3,
        out_specs=pl.BlockSpec(memory_space=pltpu.VMEM),
        scratch_shapes=[
            pltpu.VMEM((n, channels) + block, bf16),
            pltpu.VMEM((states,) + block, bf16),
            pltpu.VMEM((channels,) + block, bf16),
            pltpu.VMEM((2 * n, channels) + block, bf16),
            pltpu.VMEM((count,) + block, bf16),
            pltpu.VMEM((count,) + block, bf16),
            pltpu.VMEM((remote,) + block, bf16),
            pltpu.VMEM((remote,) + block, bf16),
            pltpu.VMEM((per,) + block, f32),
            pltpu.SemaphoreType.DMA((3,)),
            pltpu.SemaphoreType.DMA((n, channels, 4)),
            pltpu.SemaphoreType.DMA((n, channels)),
            pltpu.SemaphoreType.DMA((count,)),
            pltpu.SemaphoreType.DMA((count,)),
            pltpu.SemaphoreType.DMA((remote,)),
            pltpu.SemaphoreType.DMA((remote,)),
        ],
        compiler_params=pltpu.CompilerParams(
            collective_id=0, has_side_effects=True, vmem_limit_bytes=60 * 1024 * 1024
        ),
    )(
        right_sector.reshape(states), sector_place, left_sizes, right_sizes,
        site_operators.astype(f32).reshape(channels * states * states),
        wave_blocks.reshape((states,) + block),
        left_environment.reshape((channels,) + block),
        right_environment.reshape((channels,) + block),
    )
    return out.reshape((1, per) + block)


def solution(mesh):
    placed = (
        P("bond", None, None, None),
        P("mpo", "bond", None, None),
        P("mpo", "bond", None, None),
        P("mpo", None, None),
        P("bond", None, None),
        P(),
        P(),
        P(),
    )
    body = functools.partial(shards, mesh.shape["bond"], mesh.shape["mpo"])
    return jax.shard_map(
        body, mesh=mesh, in_specs=placed, out_specs=P("bond", "mpo", None, None), check_vma=False
    )
```

```python
import functools

import jax
import jax.numpy as jnp
from jax import lax
from jax.experimental import pallas as pl
from jax.experimental.pallas import tpu as pltpu
from jax.sharding import PartitionSpec as P

MESH = pl.DeviceIdType.MESH


def plane_of(count):
    nx = 1
    while (2 * nx) * (2 * nx) * 2 <= count and count % (2 * nx) == 0:
        nx *= 2
    return count // nx, nx


def kernel(
    n, m,
    sector, place, left_sizes, right_sizes, ops,
    wave_hbm, left_hbm, right_hbm,
    out_ref,
    right_all, wave, left, local_sem, gather_send, gather_recv, *rest,
):
    nz, nx = plane_of(n)
    cores = 2 if m % 2 == 0 else 1
    ny = m // cores
    states, rows, _ = wave.shape
    channels = left.shape[0]
    per = out_ref.shape[0]
    count = ny * per
    pair = ny == 2 and cores == 2
    if pair:
        (part, part_out, part_in, sums,
         part_send, part_recv, sum_send, sum_recv) = rest
    else:
        (mixed, out_core, in_core, out_chip, in_chip, own,
         core_send, core_recv, chip_send, chip_recv) = rest
    b = lax.axis_index("bond")
    p = lax.axis_index("mpo")
    z, x = b // nx, b % nx
    y, c = p // cores, p % cores
    sibling = y * cores + (1 - c)

    wave_copy = pltpu.make_async_copy(wave_hbm, wave, local_sem.at[0])
    left_copy = pltpu.make_async_copy(left_hbm, left, local_sem.at[1])
    own_copy = pltpu.make_async_copy(right_hbm, right_all.at[b], local_sem.at[2])
    wave_copy.start()
    left_copy.start()
    own_copy.start()

    steps = ((nx, z + 1 < nz), (-nx, z > 0), (1, x + 1 < nx), (-1, x > 0))
    barrier = pltpu.get_barrier_semaphore()
    greeted = ny
    for step, there in steps:
        greeted = greeted + there.astype(jnp.int32)

        @pl.when(there)
        def _():
            pl.semaphore_signal(barrier, inc=1, device_id=(b + step, p), device_id_type=MESH)

    pl.semaphore_signal(barrier, inc=1, device_id=(b, sibling), device_id_type=MESH)
    for dy in range(1, ny):
        other = lax.rem(y + dy, ny) * cores + c
        pl.semaphore_signal(barrier, inc=1, device_id=(b, other), device_id_type=MESH)
    pl.semaphore_wait(barrier, greeted)

    def hop(pos, h, k, src):
        return pltpu.make_async_remote_copy(
            src_ref=src,
            dst_ref=right_all.at[pos, h],
            send_sem=gather_send.at[pos, h, k],
            recv_sem=gather_recv.at[pos, h],
            device_id=(b + steps[k][0], p),
            device_id_type=MESH,
        )

    def sends(zs, xs):
        column = xs == x
        return (
            column & (zs <= z) & (z + 1 < nz),
            column & (zs >= z) & (z > 0),
            (xs <= x) & (x + 1 < nx),
            (xs >= x) & (x > 0),
        )

    def forward(zs, xs, h):
        pos = zs * nx + xs
        for k, wanted in enumerate(sends(zs, xs)):
            @pl.when(wanted)
            def _():
                hop(pos, h, k, right_all.at[pos, h]).start()

    def arrived(pos, h):
        hop(pos, h, 0, right_all.at[pos, h]).wait_recv()

    for h in range(channels):
        for k in (0, 1, 2, 3):
            @pl.when(steps[k][1])
            def _():
                hop(b, h, k, right_hbm.at[h]).start()

    wave_copy.wait()
    left_copy.wait()
    own_copy.wait()

    row_index = lax.broadcasted_iota(jnp.int32, (rows, rows), 0)
    column_index = lax.broadcasted_iota(jnp.int32, (rows, rows), 1)
    live_rows = row_index < left_sizes[b]
    op_row = lax.broadcasted_iota(jnp.int32, (states, states), 0)
    op_column = lax.broadcasted_iota(jnp.int32, (states, states), 1)

    def to_sibling(pos):
        return pltpu.make_async_remote_copy(
            src_ref=part_out.at[pos], dst_ref=part_in.at[pos],
            send_sem=part_send.at[pos], recv_sem=part_recv.at[pos],
            device_id=(b, sibling), device_id_type=MESH,
        )

    def share(kind, pos):
        source, target = (0, 0, 1)[kind], (0, 1, 1)[kind]
        device = (1 - y) * cores + c if kind == 1 else sibling
        return pltpu.make_async_remote_copy(
            src_ref=sums.at[source, pos, c], dst_ref=sums.at[target, pos, c],
            send_sem=sum_send.at[kind, pos], recv_sem=sum_recv.at[target, pos, c],
            device_id=(b, device), device_id_type=MESH,
        )

    def sum_arrived(target, pos, rank):
        pltpu.make_async_remote_copy(
            src_ref=sums.at[target, pos, rank], dst_ref=sums.at[target, pos, rank],
            send_sem=sum_send.at[0, pos], recv_sem=sum_recv.at[target, pos, rank],
            device_id=(b, sibling), device_id_type=MESH,
        ).wait_recv()

    def add_up(pos):
        to_sibling(pos).wait_recv()
        sums[0, pos, c] = (part[pos] + part_in[pos].astype(jnp.float32)).astype(jnp.bfloat16)
        share(1, pos).start()
        share(0, pos).start()

    def pass_on(pos):
        sum_arrived(1, pos, c)
        share(2, pos).start()

    def work(pos):
        def look(s, carry):
            first, last, hits = carry
            hit = place[sector[s]] == pos
            first = jnp.where(hit & (hits == 0), s, first)
            last = jnp.where(hit, s, last)
            return first, last, hits + hit.astype(jnp.int32)

        zero = jnp.int32(0)
        s1, s2, hits = lax.fori_loop(0, states, look, (zero, zero, zero), unroll=True)
        if pair:
            s1, s2 = jnp.where(c == 0, s1, s2), jnp.where(c == 0, s2, s1)
        live = live_rows & (column_index < right_sizes[sector[s1]])

        def masked(s):
            return jnp.where(live, wave[s].astype(jnp.float32), 0.0).astype(jnp.bfloat16)

        w1, w2 = masked(s1), masked(s2)
        two = hits == 2
        for h in range(channels):
            factor = right_all[pos, h]

            def right_part(w):
                part = lax.dot_general(
                    w, factor, (((1,), (1,)), ((), ())), preferred_element_type=jnp.float32
                )
                return part.astype(jnp.bfloat16).astype(jnp.float32)

            table = ops[h].astype(jnp.float32)

            def op(s, t, keep=True):
                picked = (op_row == s) & (op_column == t) & keep
                return jnp.sum(jnp.where(picked, table, 0.0), keepdims=True)

            p1, p2 = right_part(w1), right_part(w2)
            m1 = (op(s1, s1) * p1 + op(s1, s2, two) * p2).astype(jnp.bfloat16)
            m2 = (op(s2, s1, two) * p1 + op(s2, s2) * p2).astype(jnp.bfloat16)
            if pair:
                left_m = left[h]
                q1 = jnp.dot(left_m, m1, preferred_element_type=jnp.float32)
                q2 = jnp.dot(left_m, m2, preferred_element_type=jnp.float32)
                total1, total2 = (q1, q2) if h == 0 else (total1 + q1, total2 + q2)
            else:
                mixed[2 * pos, h] = m1
                mixed[2 * pos + 1, h] = m2
        if pair:
            part_out[pos] = total2.astype(jnp.bfloat16)
            to_sibling(pos).start()
            part[pos] = total1

    def gather_round(d, _):
        @pl.when((d > 0) & (d < nz))
        def _():
            for h in range(channels):
                for sign in (1, -1):
                    zs = z + sign * d

                    @pl.when((zs >= 0) & (zs < nz))
                    def _():
                        arrived(zs * nx + x, h)
                        forward(zs, x, h)

        def each(d, body):
            def one(i, _):
                sign = 1 - 2 * (i % 2)
                e = i // 2
                zs = z + sign * d
                xs = x + (e + 1) // 2 * (1 - 2 * (e % 2))

                @pl.when((zs >= 0) & (zs < nz) & (xs >= 0) & (xs < nx) & ((d > 0) | (sign > 0)))
                def _():
                    body(zs, xs)

                return 0

            lax.fori_loop(0, 2 * (2 * nx - 1), one, 0)

        def use(zs, xs):
            pos = zs * nx + xs

            @pl.when(xs != x)
            def _():
                for h in range(channels):
                    arrived(pos, h)
                    forward(zs, xs, h)

            work(pos)

        @pl.when(d <= nz)
        def _():
            each(d - 1, use)
            if pair:
                each(d - 1, lambda zs, xs: add_up(zs * nx + xs))

        if pair:
            @pl.when(d > 1)
            def _():
                each(d - 2, lambda zs, xs: pass_on(zs * nx + xs))

        return 0

    lax.fori_loop(1, nz + (2 if pair else 1), gather_round, 0)

    def rank_of(s):
        def look(t, rank):
            return rank + ((t < s) & (sector[t] == sector[s])).astype(jnp.int32)

        return jnp.minimum(lax.fori_loop(0, states, look, jnp.int32(0), unroll=True), 1)

    def finish(pos, _):
        for k, wanted in enumerate(sends(pos // nx, pos % nx)):
            @pl.when(wanted)
            def _():
                for h in range(channels):
                    hop(pos, h, k, right_all.at[pos, h]).wait_send()
        if pair:
            to_sibling(pos).wait_send()
            for kind in range(3):
                share(kind, pos).wait_send()
        return 0

    if pair:
        def all_here(pos, _):
            sum_arrived(0, pos, 1 - c)
            sum_arrived(1, pos, 1 - c)
            return 0

        lax.fori_loop(0, n, all_here, 0)
        for q in range(per):
            s = p * per + q
            at, rank = place[sector[s]], rank_of(s)
            total = sums[0, at, rank].astype(jnp.float32) + sums[1, at, rank].astype(jnp.float32)
            live = live_rows & (column_index < right_sizes[sector[s]])
            out_ref[q] = jnp.where(live, total, 0.0).astype(jnp.bfloat16)
        lax.fori_loop(0, n, finish, 0)
        return

    def product(s):
        slot = 2 * place[sector[s]] + rank_of(s)
        total = jnp.dot(left[0], mixed[slot, 0], preferred_element_type=jnp.float32)
        for h in range(1, channels):
            total += jnp.dot(left[h], mixed[slot, h], preferred_element_type=jnp.float32)
        return total

    def owner_chip(i):
        return lax.rem(y + 1 + i // per, ny)

    def to_core(i):
        return pltpu.make_async_remote_copy(
            src_ref=out_core.at[i], dst_ref=in_core.at[i],
            send_sem=core_send.at[i], recv_sem=core_recv.at[i],
            device_id=(b, sibling), device_id_type=MESH,
        )

    def to_chip(i):
        return pltpu.make_async_remote_copy(
            src_ref=out_chip.at[i], dst_ref=in_chip.at[i],
            send_sem=chip_send.at[i], recv_sem=chip_recv.at[i],
            device_id=(b, owner_chip(i) * cores + c), device_id_type=MESH,
        )

    remote = (ny - 1) * per
    lag = min(3, count)

    def reduce_step(i, _):
        @pl.when(i < count)
        def _():
            s = (owner_chip(i) * cores + (1 - c)) * per + i % per
            out_core[i] = product(s).astype(jnp.bfloat16)
            to_core(i).start()

        @pl.when(i >= lag)
        def _():
            j = i - lag
            s = (owner_chip(j) * cores + c) * per + j % per
            total = product(s)
            to_core(j).wait_recv()
            total = total + in_core[j].astype(jnp.float32)

            @pl.when(j < remote)
            def _():
                out_chip[j] = total.astype(jnp.bfloat16)
                to_chip(j).start()

            @pl.when(j >= remote)
            def _():
                own[j - remote] = total

        return 0

    lax.fori_loop(0, count + lag, reduce_step, 0)

    for q in range(per):
        total = own[q]
        for dy in range(ny - 1):
            to_chip(dy * per + q).wait_recv()
            total = total + in_chip[dy * per + q].astype(jnp.float32)
        live = live_rows & (column_index < right_sizes[sector[p * per + q]])
        out_ref[q] = jnp.where(live, total, 0.0).astype(jnp.bfloat16)

    lax.fori_loop(0, n, finish, 0)

    def finish_core(i, _):
        to_core(i).wait_send()
        return 0

    lax.fori_loop(0, count, finish_core, 0)

    def finish_chip(i, _):
        to_chip(i).wait_send()
        return 0

    lax.fori_loop(0, remote, finish_chip, 0)


def shards(n, m, wave_blocks, left_environment, right_environment, site_operators,
           right_sector, left_sizes, right_sizes, sector_place):
    states, rows = wave_blocks.shape[1:3]
    channels = left_environment.shape[0]
    per = states // m
    cores = 2 if m % 2 == 0 else 1
    ny = m // cores
    count = ny * per
    remote = max(1, (ny - 1) * per)
    block = (rows, rows)
    bf16, f32 = jnp.bfloat16, jnp.float32
    smem = pl.BlockSpec(memory_space=pltpu.SMEM)
    hbm = pl.BlockSpec(memory_space=pl.ANY)
    dma = pltpu.SemaphoreType.DMA
    if ny == 2 and cores == 2:
        rest = [
            pltpu.VMEM((n,) + block, f32),
            pltpu.VMEM((n,) + block, bf16),
            pltpu.VMEM((n,) + block, bf16),
            pltpu.VMEM((2, n, 2) + block, bf16),
            dma((n,)), dma((n,)), dma((3, n)), dma((2, n, 2)),
        ]
    else:
        rest = [
            pltpu.VMEM((2 * n, channels) + block, bf16),
            pltpu.VMEM((count,) + block, bf16),
            pltpu.VMEM((count,) + block, bf16),
            pltpu.VMEM((remote,) + block, bf16),
            pltpu.VMEM((remote,) + block, bf16),
            pltpu.VMEM((per,) + block, f32),
            dma((count,)), dma((count,)), dma((remote,)), dma((remote,)),
        ]
    out = pl.pallas_call(
        functools.partial(kernel, n, m),
        out_shape=jax.ShapeDtypeStruct((per,) + block, bf16),
        in_specs=[smem] * 4 + [pl.BlockSpec(memory_space=pltpu.VMEM)] + [hbm] * 3,
        out_specs=pl.BlockSpec(memory_space=pltpu.VMEM),
        scratch_shapes=[
            pltpu.VMEM((n, channels) + block, bf16),
            pltpu.VMEM((states,) + block, bf16),
            pltpu.VMEM((channels,) + block, bf16),
            pltpu.SemaphoreType.DMA((3,)),
            pltpu.SemaphoreType.DMA((n, channels, 4)),
            pltpu.SemaphoreType.DMA((n, channels)),
            *rest,
        ],
        compiler_params=pltpu.CompilerParams(
            collective_id=0, has_side_effects=True, vmem_limit_bytes=60 * 1024 * 1024
        ),
    )(
        right_sector.reshape(states), sector_place, left_sizes, right_sizes,
        site_operators,
        wave_blocks.reshape((states,) + block),
        left_environment.reshape((channels,) + block),
        right_environment.reshape((channels,) + block),
    )
    return out.reshape((1, per) + block)


def solution(mesh):
    placed = (
        P("bond", None, None, None),
        P("mpo", "bond", None, None),
        P("mpo", "bond", None, None),
        P("mpo", None, None),
        P("bond", None, None),
        P(),
        P(),
        P(),
    )
    body = functools.partial(shards, mesh.shape["bond"], mesh.shape["mpo"])
    return jax.shard_map(
        body, mesh=mesh, in_specs=placed, out_specs=P("bond", "mpo", None, None), check_vma=False
    )
```

```python
import functools

import jax
import jax.numpy as jnp
from jax import lax
from jax.experimental import pallas as pl
from jax.experimental.pallas import tpu as pltpu
from jax.sharding import PartitionSpec as P

MESH = pl.DeviceIdType.MESH


def plane_of(count):
    nx = 1
    while (2 * nx) * (2 * nx) * 2 <= count and count % (2 * nx) == 0:
        nx *= 2
    return count // nx, nx


def kernel(
    n, m,
    sector, place, left_sizes, right_sizes, ops,
    wave_hbm, left_hbm, right_hbm,
    out_ref,
    right_all, wave, left, local_sem, gather_send, gather_recv, *rest,
):
    nz, nx = plane_of(n)
    cores = 2 if m % 2 == 0 else 1
    ny = m // cores
    states, rows, _ = wave.shape
    channels = left.shape[0]
    per = out_ref.shape[0]
    count = ny * per
    pair = ny == 2 and cores == 2
    if pair:
        (part, part_out, part_in, sums,
         part_send, part_recv, sum_send, sum_recv) = rest
    else:
        (mixed, out_core, in_core, out_chip, in_chip, own,
         core_send, core_recv, chip_send, chip_recv) = rest
    b = lax.axis_index("bond")
    p = lax.axis_index("mpo")
    z, x = b // nx, b % nx
    y, c = p // cores, p % cores
    sibling = y * cores + (1 - c)

    wave_copy = pltpu.make_async_copy(wave_hbm, wave, local_sem.at[0])
    left_copy = pltpu.make_async_copy(left_hbm, left, local_sem.at[1])
    own_copy = pltpu.make_async_copy(right_hbm, right_all.at[b], local_sem.at[2])
    wave_copy.start()
    left_copy.start()
    own_copy.start()

    steps = ((nx, z + 1 < nz), (-nx, z > 0), (1, x + 1 < nx), (-1, x > 0))
    barrier = pltpu.get_barrier_semaphore()
    greeted = ny
    for step, there in steps:
        greeted = greeted + there.astype(jnp.int32)

        @pl.when(there)
        def _():
            pl.semaphore_signal(barrier, inc=1, device_id=(b + step, p), device_id_type=MESH)

    pl.semaphore_signal(barrier, inc=1, device_id=(b, sibling), device_id_type=MESH)
    for dy in range(1, ny):
        other = lax.rem(y + dy, ny) * cores + c
        pl.semaphore_signal(barrier, inc=1, device_id=(b, other), device_id_type=MESH)
    pl.semaphore_wait(barrier, greeted)

    def hop(pos, h, k, src):
        return pltpu.make_async_remote_copy(
            src_ref=src,
            dst_ref=right_all.at[pos, h],
            send_sem=gather_send.at[pos, h, k],
            recv_sem=gather_recv.at[pos, h],
            device_id=(b + steps[k][0], p),
            device_id_type=MESH,
        )

    def sends(zs, xs, h):
        column = xs == x
        if nx == 2 and h == channels - 1 and channels > 1:
            detour = (zs == 0) | (zs == nz - 1)
            along, across = column | detour, ~detour | (zs == z)
        else:
            along, across = column, True
        return (
            along & (zs <= z) & (z + 1 < nz),
            along & (zs >= z) & (z > 0),
            across & (xs <= x) & (x + 1 < nx),
            across & (xs >= x) & (x > 0),
        )

    def forward(zs, xs, h):
        pos = zs * nx + xs
        for k, wanted in enumerate(sends(zs, xs, h)):
            @pl.when(wanted)
            def _():
                hop(pos, h, k, right_all.at[pos, h]).start()

    def arrived(pos, h):
        hop(pos, h, 0, right_all.at[pos, h]).wait_recv()

    for h in range(channels):
        for k in (0, 1, 2, 3):
            @pl.when(steps[k][1])
            def _():
                hop(b, h, k, right_hbm.at[h]).start()

    wave_copy.wait()
    left_copy.wait()
    own_copy.wait()

    row_index = lax.broadcasted_iota(jnp.int32, (rows, rows), 0)
    column_index = lax.broadcasted_iota(jnp.int32, (rows, rows), 1)
    live_rows = row_index < left_sizes[b]
    op_row = lax.broadcasted_iota(jnp.int32, (states, states), 0)
    op_column = lax.broadcasted_iota(jnp.int32, (states, states), 1)

    def to_sibling(pos):
        return pltpu.make_async_remote_copy(
            src_ref=part_out.at[pos], dst_ref=part_in.at[pos],
            send_sem=part_send.at[pos], recv_sem=part_recv.at[pos],
            device_id=(b, sibling), device_id_type=MESH,
        )

    def share(kind, pos):
        source, target = (0, 0, 1)[kind], (0, 1, 1)[kind]
        device = (1 - y) * cores + c if kind == 1 else sibling
        return pltpu.make_async_remote_copy(
            src_ref=sums.at[source, pos, c], dst_ref=sums.at[target, pos, c],
            send_sem=sum_send.at[kind, pos], recv_sem=sum_recv.at[target, pos, c],
            device_id=(b, device), device_id_type=MESH,
        )

    def sum_arrived(target, pos, rank):
        pltpu.make_async_remote_copy(
            src_ref=sums.at[target, pos, rank], dst_ref=sums.at[target, pos, rank],
            send_sem=sum_send.at[0, pos], recv_sem=sum_recv.at[target, pos, rank],
            device_id=(b, sibling), device_id_type=MESH,
        ).wait_recv()

    def add_up(pos):
        to_sibling(pos).wait_recv()
        sums[0, pos, c] = (part[pos] + part_in[pos].astype(jnp.float32)).astype(jnp.bfloat16)
        share(1, pos).start()
        share(0, pos).start()

    def pass_on(pos):
        sum_arrived(1, pos, c)
        share(2, pos).start()

    def work(pos):
        def look(s, carry):
            first, last, hits = carry
            hit = place[sector[s]] == pos
            first = jnp.where(hit & (hits == 0), s, first)
            last = jnp.where(hit, s, last)
            return first, last, hits + hit.astype(jnp.int32)

        zero = jnp.int32(0)
        s1, s2, hits = lax.fori_loop(0, states, look, (zero, zero, zero), unroll=True)
        if pair:
            s1, s2 = jnp.where(c == 0, s1, s2), jnp.where(c == 0, s2, s1)
        live = live_rows & (column_index < right_sizes[sector[s1]])

        def masked(s):
            return jnp.where(live, wave[s].astype(jnp.float32), 0.0).astype(jnp.bfloat16)

        w1, w2 = masked(s1), masked(s2)
        two = hits == 2
        for h in range(channels):
            factor = right_all[pos, h]

            def right_part(w):
                part = lax.dot_general(
                    w, factor, (((1,), (1,)), ((), ())), preferred_element_type=jnp.float32
                )
                return part.astype(jnp.bfloat16).astype(jnp.float32)

            table = ops[h].astype(jnp.float32)

            def op(s, t, keep=True):
                picked = (op_row == s) & (op_column == t) & keep
                return jnp.sum(jnp.where(picked, table, 0.0), keepdims=True)

            p1, p2 = right_part(w1), right_part(w2)
            m1 = (op(s1, s1) * p1 + op(s1, s2, two) * p2).astype(jnp.bfloat16)
            m2 = (op(s2, s1, two) * p1 + op(s2, s2) * p2).astype(jnp.bfloat16)
            if pair:
                left_m = left[h]
                q1 = jnp.dot(left_m, m1, preferred_element_type=jnp.float32)
                q2 = jnp.dot(left_m, m2, preferred_element_type=jnp.float32)
                total1, total2 = (q1, q2) if h == 0 else (total1 + q1, total2 + q2)
            else:
                mixed[2 * pos, h] = m1
                mixed[2 * pos + 1, h] = m2
        if pair:
            part_out[pos] = total2.astype(jnp.bfloat16)
            to_sibling(pos).start()
            part[pos] = total1

    def each(g, body):
        def one(i, _):
            sign = 1 - 2 * (i % 2)
            e = i // 2
            d = g - (e > 0).astype(jnp.int32)
            zs = z + sign * d
            xs = x + (e + 1) // 2 * (1 - 2 * (e % 2))

            @pl.when((zs >= 0) & (zs < nz) & (xs >= 0) & (xs < nx) & (d >= 0) & ((d > 0) | (sign > 0)))
            def _():
                body(zs, xs)

            return 0

        lax.fori_loop(0, 2 * (2 * nx - 1), one, 0)

    def use(zs, xs):
        pos = zs * nx + xs

        @pl.when(xs != x)
        def _():
            for h in range(channels):
                arrived(pos, h)
                forward(zs, xs, h)

        work(pos)

    def gather_round(g, _):
        @pl.when((g > 0) & (g < nz))
        def _():
            for h in range(channels):
                for sign in (1, -1):
                    zs = z + sign * g

                    @pl.when((zs >= 0) & (zs < nz))
                    def _():
                        arrived(zs * nx + x, h)
                        forward(zs, x, h)

        @pl.when(g <= nz)
        def _():
            each(g, use)
            if pair:
                each(g, lambda zs, xs: add_up(zs * nx + xs))

        if pair:
            @pl.when(g > 1)
            def _():
                each(g - 2, lambda zs, xs: pass_on(zs * nx + xs))

        return 0

    lax.fori_loop(0, nz + (3 if pair else 1), gather_round, 0)

    def rank_of(s):
        def look(t, rank):
            return rank + ((t < s) & (sector[t] == sector[s])).astype(jnp.int32)

        return jnp.minimum(lax.fori_loop(0, states, look, jnp.int32(0), unroll=True), 1)

    def finish(pos, _):
        for h in range(channels):
            for k, wanted in enumerate(sends(pos // nx, pos % nx, h)):
                @pl.when(wanted)
                def _():
                    hop(pos, h, k, right_all.at[pos, h]).wait_send()
        if pair:
            to_sibling(pos).wait_send()
            for kind in range(3):
                share(kind, pos).wait_send()
        return 0

    if pair:
        def all_here(pos, _):
            sum_arrived(0, pos, 1 - c)
            sum_arrived(1, pos, 1 - c)
            return 0

        lax.fori_loop(0, n, all_here, 0)
        for q in range(per):
            s = p * per + q
            at, rank = place[sector[s]], rank_of(s)
            total = sums[0, at, rank].astype(jnp.float32) + sums[1, at, rank].astype(jnp.float32)
            live = live_rows & (column_index < right_sizes[sector[s]])
            out_ref[q] = jnp.where(live, total, 0.0).astype(jnp.bfloat16)
        lax.fori_loop(0, n, finish, 0)
        return

    def product(s):
        slot = 2 * place[sector[s]] + rank_of(s)
        total = jnp.dot(left[0], mixed[slot, 0], preferred_element_type=jnp.float32)
        for h in range(1, channels):
            total += jnp.dot(left[h], mixed[slot, h], preferred_element_type=jnp.float32)
        return total

    def owner_chip(i):
        return lax.rem(y + 1 + i // per, ny)

    def to_core(i):
        return pltpu.make_async_remote_copy(
            src_ref=out_core.at[i], dst_ref=in_core.at[i],
            send_sem=core_send.at[i], recv_sem=core_recv.at[i],
            device_id=(b, sibling), device_id_type=MESH,
        )

    def to_chip(i):
        return pltpu.make_async_remote_copy(
            src_ref=out_chip.at[i], dst_ref=in_chip.at[i],
            send_sem=chip_send.at[i], recv_sem=chip_recv.at[i],
            device_id=(b, owner_chip(i) * cores + c), device_id_type=MESH,
        )

    remote = (ny - 1) * per
    lag = min(3, count)

    def reduce_step(i, _):
        @pl.when(i < count)
        def _():
            s = (owner_chip(i) * cores + (1 - c)) * per + i % per
            out_core[i] = product(s).astype(jnp.bfloat16)
            to_core(i).start()

        @pl.when(i >= lag)
        def _():
            j = i - lag
            s = (owner_chip(j) * cores + c) * per + j % per
            total = product(s)
            to_core(j).wait_recv()
            total = total + in_core[j].astype(jnp.float32)

            @pl.when(j < remote)
            def _():
                out_chip[j] = total.astype(jnp.bfloat16)
                to_chip(j).start()

            @pl.when(j >= remote)
            def _():
                own[j - remote] = total

        return 0

    lax.fori_loop(0, count + lag, reduce_step, 0)

    for q in range(per):
        total = own[q]
        for dy in range(ny - 1):
            to_chip(dy * per + q).wait_recv()
            total = total + in_chip[dy * per + q].astype(jnp.float32)
        live = live_rows & (column_index < right_sizes[sector[p * per + q]])
        out_ref[q] = jnp.where(live, total, 0.0).astype(jnp.bfloat16)

    lax.fori_loop(0, n, finish, 0)

    def finish_core(i, _):
        to_core(i).wait_send()
        return 0

    lax.fori_loop(0, count, finish_core, 0)

    def finish_chip(i, _):
        to_chip(i).wait_send()
        return 0

    lax.fori_loop(0, remote, finish_chip, 0)


def shards(n, m, wave_blocks, left_environment, right_environment, site_operators,
           right_sector, left_sizes, right_sizes, sector_place):
    states, rows = wave_blocks.shape[1:3]
    channels = left_environment.shape[0]
    per = states // m
    cores = 2 if m % 2 == 0 else 1
    ny = m // cores
    count = ny * per
    remote = max(1, (ny - 1) * per)
    block = (rows, rows)
    bf16, f32 = jnp.bfloat16, jnp.float32
    smem = pl.BlockSpec(memory_space=pltpu.SMEM)
    hbm = pl.BlockSpec(memory_space=pl.ANY)
    dma = pltpu.SemaphoreType.DMA
    if ny == 2 and cores == 2:
        rest = [
            pltpu.VMEM((n,) + block, f32),
            pltpu.VMEM((n,) + block, bf16),
            pltpu.VMEM((n,) + block, bf16),
            pltpu.VMEM((2, n, 2) + block, bf16),
            dma((n,)), dma((n,)), dma((3, n)), dma((2, n, 2)),
        ]
    else:
        rest = [
            pltpu.VMEM((2 * n, channels) + block, bf16),
            pltpu.VMEM((count,) + block, bf16),
            pltpu.VMEM((count,) + block, bf16),
            pltpu.VMEM((remote,) + block, bf16),
            pltpu.VMEM((remote,) + block, bf16),
            pltpu.VMEM((per,) + block, f32),
            dma((count,)), dma((count,)), dma((remote,)), dma((remote,)),
        ]
    out = pl.pallas_call(
        functools.partial(kernel, n, m),
        out_shape=jax.ShapeDtypeStruct((per,) + block, bf16),
        in_specs=[smem] * 4 + [pl.BlockSpec(memory_space=pltpu.VMEM)] + [hbm] * 3,
        out_specs=pl.BlockSpec(memory_space=pltpu.VMEM),
        scratch_shapes=[
            pltpu.VMEM((n, channels) + block, bf16),
            pltpu.VMEM((states,) + block, bf16),
            pltpu.VMEM((channels,) + block, bf16),
            pltpu.SemaphoreType.DMA((3,)),
            pltpu.SemaphoreType.DMA((n, channels, 4)),
            pltpu.SemaphoreType.DMA((n, channels)),
            *rest,
        ],
        compiler_params=pltpu.CompilerParams(
            collective_id=0, has_side_effects=True, vmem_limit_bytes=60 * 1024 * 1024
        ),
    )(
        right_sector.reshape(states), sector_place, left_sizes, right_sizes,
        site_operators,
        wave_blocks.reshape((states,) + block),
        left_environment.reshape((channels,) + block),
        right_environment.reshape((channels,) + block),
    )
    return out.reshape((1, per) + block)


def solution(mesh):
    placed = (
        P("bond", None, None, None),
        P("mpo", "bond", None, None),
        P("mpo", "bond", None, None),
        P("mpo", None, None),
        P("bond", None, None),
        P(),
        P(),
        P(),
    )
    body = functools.partial(shards, mesh.shape["bond"], mesh.shape["mpo"])
    return jax.shard_map(
        body, mesh=mesh, in_specs=placed, out_specs=P("bond", "mpo", None, None), check_vma=False
    )
```

```python
import functools

import jax
import jax.numpy as jnp
from jax import lax
from jax.experimental import pallas as pl
from jax.experimental.pallas import tpu as pltpu
from jax.sharding import PartitionSpec as P

MESH = pl.DeviceIdType.MESH


def plane_of(count):
    nx = 1
    while (2 * nx) * (2 * nx) * 2 <= count and count % (2 * nx) == 0:
        nx *= 2
    return count // nx, nx


def kernel(
    n, m,
    sector, place, left_sizes, right_sizes, ops,
    wave_hbm, left_hbm, right_hbm,
    out_ref,
    right_all, wave, left, local_sem, gather_send, gather_recv, *rest,
):
    nz, nx = plane_of(n)
    cores = 2 if m % 2 == 0 else 1
    ny = m // cores
    states, rows, _ = wave.shape
    channels = left.shape[0]
    per = out_ref.shape[0]
    count = ny * per
    pair = ny == 2 and cores == 2
    if pair:
        (part, part_out, part_in, sums,
         part_send, part_recv, sum_send, sum_recv) = rest
    else:
        (mixed, out_core, in_core, out_chip, in_chip, own,
         core_send, core_recv, chip_send, chip_recv) = rest
    b = lax.axis_index("bond")
    p = lax.axis_index("mpo")
    z, x = b // nx, b % nx
    y, c = p // cores, p % cores
    sibling = y * cores + (1 - c)

    wave_copy = pltpu.make_async_copy(wave_hbm, wave, local_sem.at[0])
    left_copy = pltpu.make_async_copy(left_hbm, left, local_sem.at[1])
    own_copy = pltpu.make_async_copy(right_hbm, right_all.at[b], local_sem.at[2])
    wave_copy.start()
    left_copy.start()
    own_copy.start()

    steps = ((nx, z + 1 < nz), (-nx, z > 0), (1, x + 1 < nx), (-1, x > 0))
    barrier = pltpu.get_barrier_semaphore()
    greeted = ny
    for step, there in steps:
        greeted = greeted + there.astype(jnp.int32)

        @pl.when(there)
        def _():
            pl.semaphore_signal(barrier, inc=1, device_id=(b + step, p), device_id_type=MESH)

    pl.semaphore_signal(barrier, inc=1, device_id=(b, sibling), device_id_type=MESH)
    for dy in range(1, ny):
        other = lax.rem(y + dy, ny) * cores + c
        pl.semaphore_signal(barrier, inc=1, device_id=(b, other), device_id_type=MESH)
    pl.semaphore_wait(barrier, greeted)

    def hop(pos, h, k, src):
        return pltpu.make_async_remote_copy(
            src_ref=src,
            dst_ref=right_all.at[pos, h],
            send_sem=gather_send.at[pos, h, k],
            recv_sem=gather_recv.at[pos, h],
            device_id=(b + steps[k][0], p),
            device_id_type=MESH,
        )

    def sends(zs, xs, h):
        column = xs == x
        if nx == 2 and h == channels - 1 and channels > 1:
            detour = (zs == 0) | (zs == nz - 1)
            along, across = column | detour, ~detour | (zs == z)
        else:
            along, across = column, True
        return (
            along & (zs <= z) & (z + 1 < nz),
            along & (zs >= z) & (z > 0),
            across & (xs <= x) & (x + 1 < nx),
            across & (xs >= x) & (x > 0),
        )

    def forward(zs, xs, h):
        pos = zs * nx + xs
        for k, wanted in enumerate(sends(zs, xs, h)):
            @pl.when(wanted)
            def _():
                hop(pos, h, k, right_all.at[pos, h]).start()

    def arrived(pos, h):
        hop(pos, h, 0, right_all.at[pos, h]).wait_recv()

    for h in range(channels):
        for k in (0, 1, 2, 3):
            @pl.when(steps[k][1])
            def _():
                hop(b, h, k, right_hbm.at[h]).start()

    wave_copy.wait()
    left_copy.wait()
    own_copy.wait()

    row_index = lax.broadcasted_iota(jnp.int32, (rows, rows), 0)
    column_index = lax.broadcasted_iota(jnp.int32, (rows, rows), 1)
    live_rows = row_index < left_sizes[b]
    op_row = lax.broadcasted_iota(jnp.int32, (states, states), 0)
    op_column = lax.broadcasted_iota(jnp.int32, (states, states), 1)

    def to_sibling(pos):
        return pltpu.make_async_remote_copy(
            src_ref=part_out.at[pos], dst_ref=part_in.at[pos],
            send_sem=part_send.at[pos], recv_sem=part_recv.at[pos],
            device_id=(b, sibling), device_id_type=MESH,
        )

    def share(kind, pos):
        source, target = (0, 0, 1)[kind], (0, 1, 1)[kind]
        device = (1 - y) * cores + c if kind == 1 else sibling
        return pltpu.make_async_remote_copy(
            src_ref=sums.at[source, pos, c], dst_ref=sums.at[target, pos, c],
            send_sem=sum_send.at[kind, pos], recv_sem=sum_recv.at[target, pos, c],
            device_id=(b, device), device_id_type=MESH,
        )

    def sum_arrived(target, pos, rank):
        pltpu.make_async_remote_copy(
            src_ref=sums.at[target, pos, rank], dst_ref=sums.at[target, pos, rank],
            send_sem=sum_send.at[0, pos], recv_sem=sum_recv.at[target, pos, rank],
            device_id=(b, sibling), device_id_type=MESH,
        ).wait_recv()

    def add_up(pos):
        to_sibling(pos).wait_recv()
        sums[0, pos, c] = (part[pos] + part_in[pos].astype(jnp.float32)).astype(jnp.bfloat16)
        share(1, pos).start()
        share(0, pos).start()

    def pass_on(pos):
        sum_arrived(1, pos, c)
        share(2, pos).start()

    def work(pos):
        def look(s, carry):
            first, last, hits = carry
            hit = place[sector[s]] == pos
            first = jnp.where(hit & (hits == 0), s, first)
            last = jnp.where(hit, s, last)
            return first, last, hits + hit.astype(jnp.int32)

        zero = jnp.int32(0)
        s1, s2, hits = lax.fori_loop(0, states, look, (zero, zero, zero), unroll=True)
        if pair:
            s1, s2 = jnp.where(c == 0, s1, s2), jnp.where(c == 0, s2, s1)
        live = live_rows & (column_index < right_sizes[sector[s1]])

        def masked(s):
            return jnp.where(live, wave[s].astype(jnp.float32), 0.0).astype(jnp.bfloat16)

        both = jnp.concatenate([masked(s1), masked(s2)], axis=0)
        two = hits == 2
        for h in range(channels):
            factor = right_all[pos, h]

            parts = lax.dot_general(
                both, factor, (((1,), (1,)), ((), ())), preferred_element_type=jnp.float32
            ).astype(jnp.bfloat16).astype(jnp.float32)
            p1, p2 = parts[:rows], parts[rows:]
            table = ops[h].astype(jnp.float32)

            def op(s, t, keep=True):
                picked = (op_row == s) & (op_column == t) & keep
                return jnp.sum(jnp.where(picked, table, 0.0), keepdims=True)

            m1 = (op(s1, s1) * p1 + op(s1, s2, two) * p2).astype(jnp.bfloat16)
            m2 = (op(s2, s1, two) * p1 + op(s2, s2) * p2).astype(jnp.bfloat16)
            if pair:
                left_m = left[h]
                q1 = jnp.dot(left_m, m1, preferred_element_type=jnp.float32)
                q2 = jnp.dot(left_m, m2, preferred_element_type=jnp.float32)
                total1, total2 = (q1, q2) if h == 0 else (total1 + q1, total2 + q2)
            else:
                mixed[2 * pos, h] = m1
                mixed[2 * pos + 1, h] = m2
        if pair:
            part_out[pos] = total2.astype(jnp.bfloat16)
            to_sibling(pos).start()
            part[pos] = total1

    def at(g, i, body):
        sign = 1 - 2 * (i % 2)
        e = i // 2
        d = g - (e > 0).astype(jnp.int32)
        zs = z + sign * d
        xs = x + (e + 1) // 2 * (1 - 2 * (e % 2))

        @pl.when((zs >= 0) & (zs < nz) & (xs >= 0) & (xs < nx) & (d >= 0) & ((d > 0) | (sign > 0)))
        def _():
            body(zs, xs)

    items = 2 * (2 * nx - 1)

    def each(g, body):
        def one(i, _):
            at(g, i, body)
            return 0

        lax.fori_loop(0, items, one, 0)

    def multiply(g):
        def one(i, _):
            @pl.when(i < items)
            def _():
                at(g, i, use)

            @pl.when(i >= 2)
            def _():
                at(g, i - 2, lambda zs, xs: add_up(zs * nx + xs))

            return 0

        lax.fori_loop(0, items + 2, one, 0)

    def use(zs, xs):
        pos = zs * nx + xs

        @pl.when(xs != x)
        def _():
            for h in range(channels):
                arrived(pos, h)
                forward(zs, xs, h)

        work(pos)

    def gather_round(g, _):
        @pl.when((g > 0) & (g < nz))
        def _():
            for h in range(channels):
                for sign in (1, -1):
                    zs = z + sign * g

                    @pl.when((zs >= 0) & (zs < nz))
                    def _():
                        arrived(zs * nx + x, h)
                        forward(zs, x, h)

        @pl.when(g <= nz)
        def _():
            if pair:
                multiply(g)
            else:
                each(g, use)

        if pair:
            @pl.when(g > 1)
            def _():
                each(g - 2, lambda zs, xs: pass_on(zs * nx + xs))

        return 0

    lax.fori_loop(0, nz + (3 if pair else 1), gather_round, 0)

    def rank_of(s):
        def look(t, rank):
            return rank + ((t < s) & (sector[t] == sector[s])).astype(jnp.int32)

        return jnp.minimum(lax.fori_loop(0, states, look, jnp.int32(0), unroll=True), 1)

    def finish(pos, _):
        for h in range(channels):
            for k, wanted in enumerate(sends(pos // nx, pos % nx, h)):
                @pl.when(wanted)
                def _():
                    hop(pos, h, k, right_all.at[pos, h]).wait_send()
        if pair:
            to_sibling(pos).wait_send()
            for kind in range(3):
                share(kind, pos).wait_send()
        return 0

    if pair:
        def all_here(pos, _):
            sum_arrived(0, pos, 1 - c)
            sum_arrived(1, pos, 1 - c)
            return 0

        lax.fori_loop(0, n, all_here, 0)
        for q in range(per):
            s = p * per + q
            at, rank = place[sector[s]], rank_of(s)
            total = sums[0, at, rank].astype(jnp.float32) + sums[1, at, rank].astype(jnp.float32)
            live = live_rows & (column_index < right_sizes[sector[s]])
            out_ref[q] = jnp.where(live, total, 0.0).astype(jnp.bfloat16)
        lax.fori_loop(0, n, finish, 0)
        return

    def product(s):
        slot = 2 * place[sector[s]] + rank_of(s)
        total = jnp.dot(left[0], mixed[slot, 0], preferred_element_type=jnp.float32)
        for h in range(1, channels):
            total += jnp.dot(left[h], mixed[slot, h], preferred_element_type=jnp.float32)
        return total

    def owner_chip(i):
        return lax.rem(y + 1 + i // per, ny)

    def to_core(i):
        return pltpu.make_async_remote_copy(
            src_ref=out_core.at[i], dst_ref=in_core.at[i],
            send_sem=core_send.at[i], recv_sem=core_recv.at[i],
            device_id=(b, sibling), device_id_type=MESH,
        )

    def to_chip(i):
        return pltpu.make_async_remote_copy(
            src_ref=out_chip.at[i], dst_ref=in_chip.at[i],
            send_sem=chip_send.at[i], recv_sem=chip_recv.at[i],
            device_id=(b, owner_chip(i) * cores + c), device_id_type=MESH,
        )

    remote = (ny - 1) * per
    lag = min(3, count)

    def reduce_step(i, _):
        @pl.when(i < count)
        def _():
            s = (owner_chip(i) * cores + (1 - c)) * per + i % per
            out_core[i] = product(s).astype(jnp.bfloat16)
            to_core(i).start()

        @pl.when(i >= lag)
        def _():
            j = i - lag
            s = (owner_chip(j) * cores + c) * per + j % per
            total = product(s)
            to_core(j).wait_recv()
            total = total + in_core[j].astype(jnp.float32)

            @pl.when(j < remote)
            def _():
                out_chip[j] = total.astype(jnp.bfloat16)
                to_chip(j).start()

            @pl.when(j >= remote)
            def _():
                own[j - remote] = total

        return 0

    lax.fori_loop(0, count + lag, reduce_step, 0)

    for q in range(per):
        total = own[q]
        for dy in range(ny - 1):
            to_chip(dy * per + q).wait_recv()
            total = total + in_chip[dy * per + q].astype(jnp.float32)
        live = live_rows & (column_index < right_sizes[sector[p * per + q]])
        out_ref[q] = jnp.where(live, total, 0.0).astype(jnp.bfloat16)

    lax.fori_loop(0, n, finish, 0)

    def finish_core(i, _):
        to_core(i).wait_send()
        return 0

    lax.fori_loop(0, count, finish_core, 0)

    def finish_chip(i, _):
        to_chip(i).wait_send()
        return 0

    lax.fori_loop(0, remote, finish_chip, 0)


def shards(n, m, wave_blocks, left_environment, right_environment, site_operators,
           right_sector, left_sizes, right_sizes, sector_place):
    states, rows = wave_blocks.shape[1:3]
    channels = left_environment.shape[0]
    per = states // m
    cores = 2 if m % 2 == 0 else 1
    ny = m // cores
    count = ny * per
    remote = max(1, (ny - 1) * per)
    block = (rows, rows)
    bf16, f32 = jnp.bfloat16, jnp.float32
    smem = pl.BlockSpec(memory_space=pltpu.SMEM)
    hbm = pl.BlockSpec(memory_space=pl.ANY)
    dma = pltpu.SemaphoreType.DMA
    if ny == 2 and cores == 2:
        rest = [
            pltpu.VMEM((n,) + block, f32),
            pltpu.VMEM((n,) + block, bf16),
            pltpu.VMEM((n,) + block, bf16),
            pltpu.VMEM((2, n, 2) + block, bf16),
            dma((n,)), dma((n,)), dma((3, n)), dma((2, n, 2)),
        ]
    else:
        rest = [
            pltpu.VMEM((2 * n, channels) + block, bf16),
            pltpu.VMEM((count,) + block, bf16),
            pltpu.VMEM((count,) + block, bf16),
            pltpu.VMEM((remote,) + block, bf16),
            pltpu.VMEM((remote,) + block, bf16),
            pltpu.VMEM((per,) + block, f32),
            dma((count,)), dma((count,)), dma((remote,)), dma((remote,)),
        ]
    out = pl.pallas_call(
        functools.partial(kernel, n, m),
        out_shape=jax.ShapeDtypeStruct((per,) + block, bf16),
        in_specs=[smem] * 4 + [pl.BlockSpec(memory_space=pltpu.VMEM)] + [hbm] * 3,
        out_specs=pl.BlockSpec(memory_space=pltpu.VMEM),
        scratch_shapes=[
            pltpu.VMEM((n, channels) + block, bf16),
            pltpu.VMEM((states,) + block, bf16),
            pltpu.VMEM((channels,) + block, bf16),
            pltpu.SemaphoreType.DMA((3,)),
            pltpu.SemaphoreType.DMA((n, channels, 4)),
            pltpu.SemaphoreType.DMA((n, channels)),
            *rest,
        ],
        compiler_params=pltpu.CompilerParams(
            collective_id=0, has_side_effects=True, vmem_limit_bytes=60 * 1024 * 1024
        ),
    )(
        right_sector.reshape(states), sector_place, left_sizes, right_sizes,
        site_operators,
        wave_blocks.reshape((states,) + block),
        left_environment.reshape((channels,) + block),
        right_environment.reshape((channels,) + block),
    )
    return out.reshape((1, per) + block)


def solution(mesh):
    placed = (
        P("bond", None, None, None),
        P("mpo", "bond", None, None),
        P("mpo", "bond", None, None),
        P("mpo", None, None),
        P("bond", None, None),
        P(),
        P(),
        P(),
    )
    body = functools.partial(shards, mesh.shape["bond"], mesh.shape["mpo"])
    return jax.shard_map(
        body, mesh=mesh, in_specs=placed, out_specs=P("bond", "mpo", None, None), check_vma=False
    )
```
